32 devices in a mesh: mem: 4 (over y, core), lat: 2 (over x), lon: 4 (over z).
Axes of the slice: x: 2, y: 2, z: 4, core: 2. Of those that a mesh axis runs over, the one named last changes fastest.
Arguments:
- perturbations: bfloat16 [8, 4, 768, 1536], P('mem', None, 'lat', 'lon'), may hold values from -2 to 2
- innovation: float32 [2, 8192], P('lat', 'lon'), may hold values from -4.2 to 4.2
- obs_weight: float32 [2, 8192], P('lat', 'lon'), may hold values from 0.5 to 6, as said below
- obs_cell: int32 [2, 8192], P('lat', 'lon'), may hold values from 0 to 147455
- obs_level: int32 [2, 8192], P('lat', 'lon'), may hold values from 0 to 3
- cutoff: int32 [4], replicated, may hold values from 16 to 127
Outputs:
- solution: float32 [8, 4, 768, 512], P('mem', None, ('lat', 'lon'))
- residual: float32 [8, 4, 768, 512], P('mem', None, ('lat', 'lon'))
The draws below stay inside these ranges and needn't reach their ends.
Inputs may be any that keep to these rules, and one draw needn't show every extreme that they name: `obs_weight`: positive weights.
All inputs are finite; a program needn't handle non-finite values.
Results may differ from the reference program's by a relative error of at most 0.0008.
Values may be sent and summed in bfloat16 or wider, within the bound.
No kernel may reach another device: no remote copies, remote signals or barrier semaphores. Data moves between devices by JAX's collectives and lax.ppermute only.
A program may use at most 64 MiB of HBM per device.

```python
import jax
import jax.numpy as jnp
from jax import lax

NLAT = 768
NLON = 1536
KMAX = 256
LEV = 4
ITERS = 2
OBS_DEV = 2048
MEMBERS = 8
TILE_LAT = 384
TILE_LON = 384
N_LAT = 2
N_LON = 4


def draw_obs_weight(key, part):
    array_shape = (N_LAT, N_LON * OBS_DEV)
    first_key = jax.random.fold_in(key, 11)
    row_index = jnp.arange(N_LAT, dtype=jnp.int32)[:, None]
    col_block = jnp.arange(N_LON * OBS_DEV, dtype=jnp.int32)[None, :] // OBS_DEV
    position = (row_index * N_LON + col_block).astype(jnp.float32) / (N_LAT * N_LON - 1)
    growth_factor = 1.0 + 2.0 * position
    spread_draw = jnp.exp(jax.random.uniform(first_key, array_shape, jnp.float32, jnp.log(0.5), jnp.log(2.0)))
    return (spread_draw * growth_factor).astype(jnp.float32)


def with_ends(drawn, own_key, smallest, largest):
    longest = drawn.shape.index(max(drawn.shape))
    spots = []
    for shift in (0, 1):
        where = [jax.random.randint(jax.random.fold_in(own_key, axis), (), 0, length) for axis, length in enumerate(drawn.shape)]
        where[longest] = (where[longest] + shift) % drawn.shape[longest]
        spots.append(tuple(where))
    return drawn.at[spots[0]].set(smallest).at[spots[1]].set(largest)


def block_levels(own_key, dims, pieces, low, largest):
    gain, own = 1.0, jax.random.fold_in(own_key, 6)
    for dim, parts in pieces:
        draws = jnp.exp(jax.random.uniform(jax.random.fold_in(own, dim), (parts,), jnp.float32, low / len(pieces), largest / len(pieces)))
        gain = gain * jnp.repeat(draws, dims[dim] // parts).reshape([-1 if axis == dim else 1 for axis in range(len(dims))])
    return gain


def normal_values(stream_key, extent, spread, reach, pieces=(), kind=jnp.bfloat16):
    result = spread * jax.random.normal(stream_key, extent, jnp.float32)
    if pieces:
        result = result * block_levels(stream_key, extent, pieces, -0.22, 0.18)
    return jnp.clip(result, -reach, reach).astype(kind)


def setup_inputs(seed: int = 0) -> dict:
    streams_of = jax.random.split(jax.random.key(seed), 7)
    perturbations = normal_values(streams_of[0], (MEMBERS, LEV, NLAT, NLON), MEMBERS ** -0.5, 2.0, ((0, 4), (2, 2), (3, 4)))
    innovation = normal_values(streams_of[1], (N_LAT, N_LON * OBS_DEV), 0.7, 4.2, ((0, 2), (1, 4)), jnp.float32)
    obs_weight = draw_obs_weight(jax.random.fold_in(streams_of[6], 71), 0)
    obs_cell = with_ends(jax.random.randint(streams_of[3], (N_LAT, N_LON * OBS_DEV), 0, TILE_LAT * TILE_LON), jax.random.fold_in(streams_of[3], 1), 0, (TILE_LAT * TILE_LON) - 1).astype(jnp.int32)
    obs_level = with_ends(jax.random.randint(streams_of[4], (N_LAT, N_LON * OBS_DEV), 0, LEV), jax.random.fold_in(streams_of[4], 1), 0, LEV - 1).astype(jnp.int32)
    cutoff = with_ends(jax.random.randint(streams_of[5], (LEV,), KMAX // 16, KMAX // 2), jax.random.fold_in(streams_of[5], 1), KMAX // 16, (KMAX // 2) - 1).astype(jnp.int32)
    return dict(perturbations=perturbations, innovation=innovation, obs_weight=obs_weight, obs_cell=obs_cell, obs_level=obs_level, cutoff=cutoff)


def basis_table():
    columns = jnp.arange(NLON, dtype=jnp.int32)[:, None]
    cos_waves = jnp.arange(KMAX, dtype=jnp.int32)[None, :]
    sin_waves = cos_waves + 1
    factor = 2.0 * jnp.pi / NLON
    cos_phase = (columns * cos_waves % NLON).astype(jnp.float32) * factor
    sin_phase = (columns * sin_waves % NLON).astype(jnp.float32) * factor
    joined = jnp.concatenate([jnp.cos(cos_phase), jnp.sin(sin_phase)], axis=1)
    return (joined / jnp.sqrt(jnp.float32(KMAX))).astype(jnp.float32)

def spectrum_of(cutoff):
    wavenumbers = jnp.concatenate([jnp.arange(KMAX, dtype=jnp.float32), jnp.arange(1, KMAX + 1, dtype=jnp.float32)])
    scaled = wavenumbers[None, :] / cutoff.astype(jnp.float32)[:, None]
    return 1.0 / (1.0 + scaled * scaled)

def reference(perturbations, innovation, obs_weight, obs_cell, obs_level, cutoff):
    basis = basis_table()
    spectrum = spectrum_of(cutoff)
    row_index = jnp.arange(N_LAT, dtype=jnp.int32)[:, None] * TILE_LAT + obs_cell // TILE_LON
    col_index = jnp.arange(N_LON * OBS_DEV, dtype=jnp.int32)[None, :] // OBS_DEV * TILE_LON + obs_cell % TILE_LON
    located = ((obs_level * NLAT + row_index) * NLON + col_index).reshape(-1).astype(jnp.int32)
    weights = obs_weight.reshape(-1)

    def gridded_of(weighted):
        field = jnp.zeros((LEV * NLAT * NLON,), jnp.float32).at[located].add(weighted)
        return field.reshape(LEV, NLAT, NLON)

    def synthesize(control):

        def one_member(carry, paired):
            member_pert, member_ctrl = paired
            coeffs = member_ctrl * spectrum[:, None, :]
            synthesized = jnp.dot(coeffs.reshape(-1, 2 * KMAX), basis.T, precision=lax.Precision.HIGHEST, preferred_element_type=jnp.float32)
            synthesized = synthesized.reshape(LEV, NLAT, NLON)
            return (carry + member_pert.astype(jnp.float32) * synthesized, None)
        total, unused = lax.scan(one_member, jnp.zeros((LEV, NLAT, NLON), jnp.float32), (perturbations, control))
        return total

    def analyse(gridded):

        def one_member(member_pert):
            products = member_pert.astype(jnp.float32) * gridded
            summed = jnp.dot(products.reshape(-1, NLON), basis, precision=lax.Precision.HIGHEST, preferred_element_type=jnp.float32)
            return summed.reshape(LEV, NLAT, 2 * KMAX) * spectrum[:, None, :]
        return lax.map(one_member, perturbations)

    def hessian(direction):
        increment = synthesize(direction)
        sampled = increment.reshape(-1)[located]
        return direction + analyse(gridded_of(weights * sampled))
    right_side = analyse(gridded_of(weights * innovation.reshape(-1)))
    solution = jnp.zeros_like(right_side)
    residual = right_side
    direction = right_side
    norm_now = jnp.sum(residual * residual)
    for iteration in range(ITERS):
        image = hessian(direction)
        step_size = norm_now / jnp.sum(direction * image)
        solution = solution + step_size * direction
        residual = residual - step_size * image
        norm_next = jnp.sum(residual * residual)
        direction = residual + norm_next / norm_now * direction
        norm_now = norm_next
    return (solution, residual)
```

```python
import functools

import jax
import jax.numpy as jnp
import numpy as np
from jax import lax
from jax.experimental import pallas as pl
from jax.experimental.pallas import tpu as pltpu
from jax.sharding import PartitionSpec as P

NLON = 1536
KMAX = 256
LANES = 128
BLOCK = 256
F32 = jnp.float32
BF16 = jnp.bfloat16
VMEM = pl.BlockSpec(memory_space=pltpu.VMEM)
SMEM = pl.BlockSpec(memory_space=pltpu.SMEM)


def spectrum_of(cutoff):
    wavenumbers = jnp.concatenate([jnp.arange(KMAX, dtype=F32), jnp.arange(1, KMAX + 1, dtype=F32)])
    scaled = wavenumbers[None, :] / cutoff.astype(F32)[:, None]
    return 1.0 / (1.0 + scaled * scaled)


def correlation_table(spectrum, lags):
    waves = jnp.arange(KMAX, dtype=jnp.int32)[:, None]
    phase = (waves * jnp.arange(lags, dtype=jnp.int32)[None, :] % NLON).astype(F32) * (2.0 * jnp.pi / NLON)
    power = spectrum[:, :KMAX] * spectrum[:, :KMAX] / KMAX
    return jnp.dot(power, jnp.cos(phase), precision=lax.Precision.HIGHEST, preferred_element_type=F32)


def spread(value, axis):
    size, here = lax.axis_size(axis), lax.axis_index(axis)
    if size > 8 or size & (size - 1):
        return lax.all_gather(value, axis), jnp.arange(size, dtype=jnp.int32)
    parts = [value]
    for flip in range(1, size):
        parts.append(lax.ppermute(value, axis, [(i, i ^ flip) for i in range(size)]))
    return jnp.stack(parts), here ^ jnp.arange(size, dtype=jnp.int32)


def all_members(value):
    size = lax.axis_size("mem")
    if size & (size - 1):
        gathered = lax.all_gather(value, "mem")
        return jnp.roll(gathered, -lax.axis_index("mem"), axis=0).reshape((-1,) + value.shape[1:])
    flip = 1
    while flip < size:
        value = jnp.concatenate([value, lax.ppermute(value, "mem", [(i, i ^ flip) for i in range(size)])])
        flip *= 2
    return value


def pick_kernel(col_ref, key_ref, pert_ref, out_ref, hot_ref):
    tile_rows, tile_cols = pert_ref.shape[2:]
    chunks = col_ref.shape[0]

    @pl.when((pl.program_id(0) == 0) & (pl.program_id(1) == 0))
    def _():
        for q in range(chunks):
            sub = lax.broadcasted_iota(jnp.int32, (tile_cols, LANES), 0)
            hot = jnp.where(sub == col_ref[q : q + 1, :], 1.0, 0.0)
            hot_ref[:, q * LANES : (q + 1) * LANES] = hot.astype(BF16)

    @pl.when(pl.program_id(1) == 0)
    def _():
        out_ref[...] = jnp.zeros_like(out_ref)

    block = pert_ref[0, 0]
    rows = lax.broadcasted_iota(jnp.int32, (tile_rows, LANES), 0) + pl.program_id(1) * tile_rows
    for q in range(0, chunks, 2):
        lines = jnp.dot(block, hot_ref[:, q * LANES : (q + 2) * LANES], preferred_element_type=F32)
        for h in range(2):
            mine = lines[:, h * LANES : (h + 1) * LANES]
            kept = jnp.where(rows == key_ref[q + h : q + h + 1, :], mine, 0.0)
            out_ref[0, q + h : q + h + 1, :] += jnp.sum(kept, axis=0, keepdims=True)


def pick(perturbations, col, key):
    members, levels, tile_rows, tile_cols = perturbations.shape
    chunks = col.shape[0]
    whole = pl.BlockSpec((chunks, LANES), lambda m, l: (0, 0))
    return pl.pallas_call(
        pick_kernel,
        grid=(members, levels),
        in_specs=[whole, whole, pl.BlockSpec((1, 1, tile_rows, tile_cols), lambda m, l: (m, l, 0, 0))],
        out_specs=pl.BlockSpec((1, chunks, LANES), lambda m, l: (m, 0, 0)),
        out_shape=jax.ShapeDtypeStruct((members, chunks, LANES), F32),
        scratch_shapes=[pltpu.VMEM((tile_cols, chunks * LANES), BF16)],
        name="pick",
    )(col, key, perturbations)


def take_row(row, index):
    return jnp.take_along_axis(
        jnp.broadcast_to(row, (8, LANES)), index, axis=1, mode="promise_in_bounds"
    )


def krylov_kernel(
    shift, own, line_rows, levels, per_level,
    key_ref, early_ref, pert_ref, table_ref, edge_ref,
    rows_ref, moment_ref,
    base_ref, ext_ref, pairs_ref, t_ref, acc_ref,
):
    slots, members, chunks = pert_ref.shape[:3]
    sources = key_ref.shape[0]
    bands = levels * line_rows
    fields = 5 + members
    KEY, COL, EDGE, YY, WW = 0, 1, 2, 3, 4

    count = jnp.sum(jnp.where(key_ref[...] < (bands << shift), 1.0, 0.0)).astype(jnp.int32)
    vregs = jnp.maximum((count + 8 * LANES - 1) // (8 * LANES), 1)
    depth = vregs * 8
    sub = lax.broadcasted_iota(jnp.int32, (8, LANES), 0)
    lane = lax.broadcasted_iota(jnp.int32, (8, LANES), 1)
    zero = jnp.zeros((8, LANES), F32)

    def load_sorted(v, carry):
        place = lane * depth + v * 8 + sub
        high, low = place >> 7, place & (LANES - 1)

        def key_step(r, found):
            return jnp.where(high == r, take_row(key_ref[pl.ds(r, 1), :], low), found)

        key = lax.fori_loop(0, depth, key_step, jnp.full((8, LANES), bands << shift, jnp.int32))
        inside = place < count
        band = key >> shift
        index = key & ((1 << shift) - 1)
        high, low = index >> 7, index & (LANES - 1)

        def slot_step(t, found):
            for q in range(chunks):
                here = high == t * chunks + q
                rows = [early_ref[t, k, q : q + 1, :] for k in range(3)]
                rows += [pert_ref[t, m, q : q + 1, :] for m in range(members)]
                found = tuple(jnp.where(here, take_row(row, low), f) for row, f in zip(rows, found))
            return found

        found = lax.fori_loop(0, slots, slot_step, (zero,) * (3 + members))
        level = jnp.zeros((8, LANES), jnp.int32)
        for l in range(1, levels):
            level += jnp.where(band >= l * line_rows, 1, 0)
        col, innov, weight = found[:3]
        col_int = col.astype(jnp.int32)
        wave = KMAX * col_int
        turn = (wave - (wave // NLON) * NLON).astype(F32) * (2.0 * np.pi / NLON)
        scale = zero
        for l in range(levels):
            scale = jnp.where(level == l, edge_ref[l : l + 1, :], scale)
        at = pl.ds(v * 8, 8)
        base_ref[KEY, at, :] = band.astype(F32)
        base_ref[COL, at, :] = col
        base_ref[EDGE, at, :] = jnp.where(inside, jnp.sin(turn) * scale, 0.0)
        base_ref[YY, at, :] = jnp.where(inside, weight * innov, 0.0)
        base_ref[WW, at, :] = jnp.where(inside, weight, 0.0)
        for m in range(members):
            base_ref[5 + m, at, :] = jnp.where(inside, found[3 + m], 0.0)
        pairs_ref[at, :] = level * per_level
        return carry

    lax.fori_loop(0, vregs, load_sorted, 0)

    def next_lane(x):
        return jnp.where(lane == LANES - 1, 0.0, pltpu.roll(x, LANES - 1, 1))

    def apply(target):
        def fill(v, carry):
            at, beyond = pl.ds(v * 8, 8), pl.ds(depth + v * 8, 8)
            for f in range(fields):
                value = base_ref[f, at, :]
                ext_ref[f, at, :] = value
                ext_ref[f, beyond, :] = next_lane(value)
            t_ref[target, at, :] = zero
            return carry

        lax.fori_loop(0, vregs, fill, 0)

        def lap(state):
            turns, going = state

            def clear(v, carry):
                acc_ref[pl.ds(v * 8, 8), :] = zero
                acc_ref[pl.ds(depth + v * 8, 8), :] = zero
                return carry

            lax.fori_loop(0, vregs, clear, 0)

            def batch(state):
                start, going = state

                def one(v, hit):
                    at = pl.ds(v * 8, 8)
                    mine = [base_ref[f, at, :] for f in range(fields)]
                    chunk = pairs_ref[at, :]
                    total = t_ref[target, at, :]
                    for b in range(8):
                        there = pl.ds(start + b + v * 8, 8)
                        other = [ext_ref[f, there, :] for f in range(fields)]
                        same = mine[KEY] == other[KEY]
                        lag = jnp.abs(mine[COL] - other[COL]).astype(jnp.int32)
                        lag = jnp.minimum(lag, NLON - lag)
                        which = chunk + (lag >> 7)
                        low = lag & (LANES - 1)
                        value = zero
                        for e in range(levels * per_level):
                            value = jnp.where(which == e, take_row(table_ref[e : e + 1, :], low), value)
                        value += mine[EDGE] * other[EDGE]
                        weight = mine[5] * other[5]
                        for m in range(1, members):
                            weight += mine[5 + m] * other[5 + m]
                        value = jnp.where(same, value * weight, 0.0)
                        total += value * other[YY]
                        first = (turns == 0) & (start + b == 0)
                        back = value * mine[YY] * jnp.where(first, 0.0, 1.0)
                        acc_ref[there, :] += back
                        if b == 7:
                            hit = jnp.maximum(hit, jnp.where(same & (mine[KEY] < bands), 1.0, 0.0))
                    t_ref[target, at, :] = total
                    return hit

                hit = lax.fori_loop(0, vregs, one, zero)
                return start + 8, jnp.max(hit) > 0.5

            _, going = lax.while_loop(lambda s: (s[0] < depth) & s[1], batch, (0, going))

            def fold(v, carry):
                at, beyond = pl.ds(v * 8, 8), pl.ds(depth + v * 8, 8)
                t_ref[target, at, :] += pltpu.roll(acc_ref[at, :], turns, 1) + pltpu.roll(
                    acc_ref[beyond, :], turns + 1, 1
                )
                for f in range(fields):
                    for rows in (at, beyond):
                        ext_ref[f, rows, :] = next_lane(ext_ref[f, rows, :])
                return carry

            lax.fori_loop(0, vregs, fold, 0)
            return turns + 1, going

        lax.while_loop(lambda s: (s[0] < LANES - 1) & s[1], lap, (0, True))

    apply(0)

    def middle(v, carry):
        at = pl.ds(v * 8, 8)
        t_ref[2, at, :] = base_ref[YY, at, :]
        base_ref[YY, at, :] = base_ref[WW, at, :] * t_ref[0, at, :]
        return carry

    lax.fori_loop(0, vregs, middle, 0)
    apply(1)

    def products(v, sums):
        at = pl.ds(v * 8, 8)
        y0, y1 = t_ref[2, at, :], base_ref[YY, at, :]
        t0, t1 = t_ref[0, at, :], t_ref[1, at, :]
        y2 = base_ref[WW, at, :] * t1
        t_ref[3, at, :] = y2
        return sums[0] + y0 * t0, sums[1] + y0 * t1, sums[2] + y1 * t1, sums[3] + y2 * t1

    sums = lax.fori_loop(0, vregs, products, (zero,) * 4)
    moment_ref[...] = jnp.concatenate(
        [jnp.sum(s, axis=0, keepdims=True) for s in sums] + [jnp.zeros((4, LANES), F32)]
    )

    def unload(v, carry):
        place = (v * 8 + sub) * LANES + lane
        column = jnp.floor((place.astype(F32) + 0.5) / depth.astype(F32)).astype(jnp.int32)
        column = jnp.minimum(column, LANES - 1)
        row = place - column * depth

        def step(r, found):
            here = row == r
            at = pl.ds(r, 1)
            rows = [base_ref[COL, at, :]] + [base_ref[5 + m, at, :] for m in range(own)]
            rows += [t_ref[2, at, :], base_ref[YY, at, :], t_ref[3, at, :]]
            return tuple(jnp.where(here, take_row(r_, column), f) for r_, f in zip(rows, found))

        found = lax.fori_loop(0, depth, step, (zero,) * (4 + own))
        for f, value in enumerate(found):
            rows_ref[f, pl.ds(v * 8, 8), :] = value
        return carry

    lax.fori_loop(0, vregs, unload, 0)


def krylov(keys, early, pert, table, edge, shift, own, line_rows, levels):
    slots, members, chunks = pert.shape[:3]
    sources = keys.shape[0]
    fields = 5 + members
    per_level = table.shape[0] // levels
    return pl.pallas_call(
        functools.partial(krylov_kernel, shift, own, line_rows, levels, per_level),
        in_specs=[VMEM] * 5,
        out_specs=[VMEM] * 2,
        out_shape=[
            jax.ShapeDtypeStruct((4 + own, sources, LANES), F32),
            jax.ShapeDtypeStruct((8, LANES), F32),
        ],
        scratch_shapes=[
            pltpu.VMEM((fields, sources, LANES), F32),
            pltpu.VMEM((fields, 2 * sources + 8, LANES), F32),
            pltpu.VMEM((sources, LANES), jnp.int32),
            pltpu.VMEM((4, sources, LANES), F32),
            pltpu.VMEM((2 * sources + 8, LANES), F32),
        ],
        name="krylov",
    )(keys, early, pert, table, edge)


def halves(value):
    high = value.astype(BF16)
    return high, (value - high.astype(F32)).astype(BF16)


def expand_kernel(
    shift, own, bands, chunk,
    skey_ref, key_ref, rows_ref, moment_ref, spec_ref, sol_ref, res_ref,
):
    def total(i):
        lanes = jnp.sum(moment_ref[:, i, :], axis=0, keepdims=True)
        return jnp.broadcast_to(jnp.sum(lanes, axis=1, keepdims=True), (1, LANES))

    m0, m1, m2, m3 = (total(i) for i in range(4))
    step0 = m0 / (m0 + m1)
    keep = 1.0 - step0
    next_norm = keep * keep * m0 - 2.0 * keep * step0 * m1 + step0 * step0 * m2
    ratio = next_norm / m0
    u, v = keep + ratio, -step0
    curvature = u * u * m0 + (2.0 * u * v + u * u) * m1 + (2.0 * u * v + v * v) * m2 + v * v * m3
    step1 = next_norm / curvature
    sol_c = (step0 + step1 * u, step1 * v)
    res_c = (keep - step1 * u, -step0 - step1 * (u + v), -step1 * v)

    count = jnp.sum(jnp.where(key_ref[...] < (bands << shift), 1.0, 0.0)).astype(jnp.int32)
    sol_ref[...] = jnp.zeros_like(sol_ref)
    res_ref[...] = jnp.zeros_like(res_ref)
    per = BLOCK // LANES
    wide = 2 * KMAX
    wave_row = lax.broadcasted_iota(jnp.int32, (wide, BLOCK), 0)
    wave = jnp.where(wave_row < KMAX, wave_row, wave_row - (KMAX - 1)).astype(F32)
    offset = jnp.where(wave_row < KMAX, 0.0, NLON / 4)

    def block(p, carry):
        def lanes(get):
            return jnp.concatenate([get(p * per + i) for i in range(per)], axis=1)

        def field(f):
            return lanes(lambda i: rows_ref[f, pl.ds(i, 1), :])

        place = lax.broadcasted_iota(jnp.int32, (1, BLOCK), 1) + p * BLOCK
        inside = place < count
        band = lanes(lambda i: key_ref[pl.ds(i, 1), :]) >> shift
        col = jnp.where(inside, field(0), 0.0)
        y0, y1, y2 = (field(1 + own + k) for k in range(3))
        wider = lambda c: jnp.concatenate([c] * per, axis=1)
        sol_y = wider(sol_c[0]) * y0 + wider(sol_c[1]) * y1
        res_y = wider(res_c[0]) * y0 + wider(res_c[1]) * y1 + wider(res_c[2]) * y2
        coefs = []
        for y in (sol_y, res_y):
            for m in range(own):
                coefs.append(halves(jnp.where(inside, field(1 + m) * y, 0.0)))

        phase = col * wave - offset
        phase = phase - NLON * jnp.round(phase * (1.0 / NLON))
        x = (NLON / 4 - jnp.abs(phase)) * (2.0 * np.pi / NLON)
        x2 = x * x
        poly = -2.5052108e-8
        for coefficient in (2.7557319e-6, -1.9841270e-4, 8.3333333e-3, -1.6666667e-1, 1.0):
            poly = poly * x2 + coefficient
        high, low = halves(x * poly)
        basis = jnp.concatenate([high, high, low], axis=1)

        first = skey_ref[p * BLOCK] >> shift
        last = skey_ref[jnp.minimum(p * BLOCK + BLOCK, count) - 1] >> shift

        def strip(g, carry):
            rows = lax.broadcasted_iota(jnp.int32, (chunk, BLOCK), 0) + g * chunk
            hit = rows == band

            def spot(part):
                return jnp.where(hit, part.astype(F32), 0.0)

            left_high = jnp.concatenate([spot(c[0]) for c in coefs], axis=0).astype(BF16)
            left_low = jnp.concatenate([spot(c[1]) for c in coefs], axis=0).astype(BF16)
            left = jnp.concatenate([left_high, left_low, left_high], axis=1)
            lines = lax.dot_general(
                left, basis, (((1,), (1,)), ((), ())), preferred_element_type=F32
            )
            at = pl.ds(pl.multiple_of(g * chunk, 8), chunk)
            for k in range(2 * own):
                out = sol_ref if k < own else res_ref
                out[k % own, at, :] += lines[k * chunk : (k + 1) * chunk]
            return carry

        lax.fori_loop(first // chunk, last // chunk + 1, strip, 0)
        return carry

    lax.fori_loop(0, (count + BLOCK - 1) // BLOCK, block, 0)
    for out in (sol_ref, res_ref):
        for m in range(own):
            out[m] = out[m] * spec_ref[...]


def expand(keys, rows, moments, spec, shift, own, bands, chunk):
    padded = spec.shape[0]
    return pl.pallas_call(
        functools.partial(expand_kernel, shift, own, bands, chunk),
        in_specs=[SMEM] + [VMEM] * 4,
        out_specs=[VMEM] * 2,
        out_shape=[jax.ShapeDtypeStruct((own, padded, 2 * KMAX), F32)] * 2,
        name="expand",
    )(keys.reshape(-1), keys, rows, moments, spec)


def body(perturbations, innovation, obs_weight, obs_cell, obs_level, cutoff):
    own, levels, tile_rows, tile_cols = perturbations.shape
    here = lax.axis_index("lon")
    line_rows = tile_rows // lax.axis_size("lon")
    bands = levels * line_rows
    flat = obs_cell.size
    padding = -flat % BLOCK
    cell = jnp.pad(obs_cell.reshape(-1), (0, padding)).reshape(-1, LANES)
    level = jnp.pad(obs_level.reshape(-1), (0, padding)).reshape(-1, LANES)
    innov = jnp.pad(innovation.reshape(-1), (0, padding)).reshape(-1, LANES)
    weight = jnp.pad(obs_weight.reshape(-1), (0, padding)).reshape(-1, LANES)
    line = cell // tile_cols
    col = cell - line * tile_cols
    key = level * tile_rows + line

    early = jnp.stack([col.astype(F32), innov, weight, key.astype(F32)])
    early, tiles = spread(early, "lon")
    picked = pick(perturbations, col, key)
    pert, _ = spread(all_members(picked), "lon")

    early = early.at[:, 0].add((tiles * tile_cols).astype(F32)[:, None, None])
    key = early[:, 3].astype(jnp.int32)
    key_level = key // tile_rows
    key_line = key - key_level * tile_rows - here * line_rows
    index = jnp.arange(key.size, dtype=jnp.int32).reshape(key.shape)
    shift = (key.size - 1).bit_length()
    inside = (key_line >= 0) & (key_line < line_rows)
    if padding:
        inside &= index % (flat + padding) < flat
    band = jnp.where(inside, key_level * line_rows + key_line, bands)
    keys = lax.sort(((band << shift) | index).reshape(-1)).reshape(-1, LANES)

    spectrum = spectrum_of(cutoff)
    per_level = (NLON // 2) // LANES + 1
    table = correlation_table(spectrum, per_level * LANES).reshape(-1, LANES)
    edge = jnp.broadcast_to(spectrum[:, -1:] / np.sqrt(KMAX), (levels, LANES))
    rows, moment = krylov(keys, early, pert, table, edge, shift, own, line_rows, levels)

    groups = lax.axis_size("lat") * lax.axis_size("lon")
    if groups > 16:
        moments = lax.psum(moment, ("lat", "lon"))[None]
    else:
        moments = lax.all_to_all(
            jnp.broadcast_to(moment[None], (groups,) + moment.shape), ("lat", "lon"), 0, 0, tiled=True
        )
    chunk = min(64, -(-bands // 16) * 16)
    padded = -(-bands // chunk) * chunk
    spec = jnp.repeat(spectrum / np.sqrt(KMAX), line_rows, axis=0)
    spec = jnp.pad(spec, ((0, padded - bands), (0, 0)))
    outs = expand(keys, rows, moments, spec, shift, own, bands, chunk)
    return tuple(o[:, :bands].reshape(own, levels, line_rows, 2 * KMAX) for o in outs)


def solution(mesh):
    placed = (
        P("mem", None, "lat", "lon"),
        P("lat", "lon"),
        P("lat", "lon"),
        P("lat", "lon"),
        P("lat", "lon"),
        P(),
    )
    return jax.shard_map(
        body,
        mesh=mesh,
        in_specs=placed,
        out_specs=(P("mem", None, ("lat", "lon"), None), P("mem", None, ("lat", "lon"), None)),
        check_vma=False,
    )
```

```python
import functools

import jax
import jax.numpy as jnp
import numpy as np
from jax import lax
from jax.experimental import pallas as pl
from jax.experimental.pallas import tpu as pltpu
from jax.sharding import PartitionSpec as P


NLON = 1536
KMAX = 256
LANES = 128
BLOCK = 256
KEPT = 24
F32 = jnp.float32
BF16 = jnp.bfloat16
VMEM = pl.BlockSpec(memory_space=pltpu.VMEM)
SMEM = pl.BlockSpec(memory_space=pltpu.SMEM)


def flipped(value, axis, flip):
    pairs = [(i, i ^ flip) for i in range(lax.axis_size(axis))]
    return lax.ppermute(value, axis, pairs)


def by_flips(axis):
    size = lax.axis_size(axis)
    return size <= 8 and not size & (size - 1)


def spread(value, axis):
    value = value[None]
    if not by_flips(axis):
        return [lax.all_gather(value, axis, tiled=True)]
    flips = range(1, lax.axis_size(axis))
    return [value] + [flipped(value, axis, flip) for flip in flips]


def all_members(value):
    if not by_flips("mem"):
        return list(jnp.roll(lax.all_gather(value, "mem"), -lax.axis_index("mem"), axis=0))
    stacks, flip = [value], 1
    while flip < lax.axis_size("mem"):
        stacks += [flipped(s, "mem", flip) for s in stacks]
        flip *= 2
    return stacks


def cosine(phase):
    phase = phase - NLON * jnp.round(phase * (1.0 / NLON))
    x = (NLON / 4 - jnp.abs(phase)) * (2.0 * np.pi / NLON)
    x2 = x * x
    poly = -2.5052108e-8
    for coefficient in (2.7557319e-6, -1.9841270e-4, 8.3333333e-3, -1.6666667e-1, 1.0):
        poly = poly * x2 + coefficient
    return x * poly


def cos_sin(column, wave):
    phase = column * wave
    return cosine(phase), cosine(phase - NLON / 4)


def keys_kernel(shift, flat, levels, tile_rows, line_rows, *refs):
    keys_ref = refs[-1]
    chunks = refs[0].shape[2]
    bands = levels * line_rows
    low = lax.axis_index("lon") * line_rows
    spot = lax.broadcasted_iota(jnp.int32, (chunks, LANES), 0) * LANES
    spot += lax.broadcasted_iota(jnp.int32, (chunks, LANES), 1)
    slot = 0
    for ref in refs[:-1]:

        def fill(t, carry, slot=slot, ref=ref):
            line = ref[t, 3].astype(jnp.int32)
            level = jnp.zeros_like(line)
            for l in range(1, levels):
                level += jnp.where(line >= l * tile_rows, 1, 0)
            line = line - level * tile_rows - low
            inside = (line >= 0) & (line < line_rows) & (spot < flat)
            band = jnp.where(inside, level * line_rows + line, bands)
            at = pl.ds((slot + t) * chunks, chunks)
            keys_ref[at, :] = (band << shift) + (spot + (slot + t) * (chunks * LANES))
            return carry

        if ref.shape[0] == 1:
            fill(0, 0)
        else:
            lax.fori_loop(0, ref.shape[0], fill, 0)
        slot += ref.shape[0]


def sort_keys(spread_out, shift, flat, levels, tile_rows, line_rows):
    chunks = spread_out[0].shape[2]
    slots = sum(e.shape[0] for e in spread_out)
    return pl.pallas_call(
        functools.partial(keys_kernel, shift, flat, levels, tile_rows, line_rows),
        in_specs=[VMEM] * len(spread_out),
        out_specs=VMEM,
        out_shape=jax.ShapeDtypeStruct((slots * chunks, LANES), jnp.int32),
        name="keys",
    )(*spread_out)


def tables_kernel(cutoff_ref, spec_ref, table_ref, trig_ref):
    levels, lags = table_ref.shape
    scales = [cutoff_ref[l].astype(F32) for l in range(levels)]
    wide = lax.broadcasted_iota(jnp.int32, (1, 2 * KMAX), 1)
    wave = jnp.where(wide < KMAX, wide, wide - (KMAX - 1)).astype(F32)
    for l in range(levels):
        scaled = wave / scales[l]
        spec_ref[l : l + 1, :] = 1.0 / (1.0 + scaled * scaled)

    lag = lax.broadcasted_iota(jnp.int32, (1, lags), 1).astype(F32)
    leaps = lax.broadcasted_iota(jnp.int32, (KMAX // 8, lags), 0).astype(F32) * 8.0
    for part, value in enumerate(cos_sin(lag, leaps)):
        for k in range(lags // LANES):
            trig_ref[part, k] = value[:, k * LANES : (k + 1) * LANES]
    near_cos, near_sin = cos_sin(lag, lax.broadcasted_iota(jnp.int32, (8, lags), 0).astype(F32))
    row = lax.broadcasted_iota(jnp.int32, (8, LANES), 0).astype(F32)

    def add(a, sums):
        far = pl.ds(a, 1)
        wave = row + (a * 8).astype(F32)
        powers = []
        for l in range(levels):
            scaled = wave / scales[l]
            value = 1.0 / (1.0 + scaled * scaled)
            powers.append(value * value)
        sums = list(sums)
        for k in range(lags // LANES):
            at = slice(k * LANES, (k + 1) * LANES)
            value = trig_ref[0, k, far, :] * near_cos[:, at] - trig_ref[1, k, far, :] * near_sin[:, at]
            for l in range(levels):
                e = l * (lags // LANES) + k
                sums[e] = sums[e] + powers[l] * value
        return tuple(sums)

    zero = jnp.zeros((8, LANES), F32)
    sums = lax.fori_loop(0, KMAX // 8, add, (zero,) * (levels * lags // LANES))
    for e, total in enumerate(sums):
        l, k = divmod(e, lags // LANES)
        total = jnp.sum(total, axis=0, keepdims=True) * (1.0 / KMAX)
        table_ref[l : l + 1, k * LANES : (k + 1) * LANES] = total


def tables(cutoff):
    levels = cutoff.shape[0]
    lags = (NLON // 2 // LANES + 1) * LANES
    return pl.pallas_call(
        tables_kernel,
        in_specs=[SMEM],
        out_specs=[VMEM] * 2,
        out_shape=[
            jax.ShapeDtypeStruct((levels, 2 * KMAX), F32),
            jax.ShapeDtypeStruct((levels, lags), F32),
        ],
        scratch_shapes=[pltpu.VMEM((2, lags // LANES, KMAX // 8, LANES), F32)],
        name="tables",
    )(cutoff)


def split_kernel(tile_rows, tile_cols, innov_ref, weight_ref, cell_ref, level_ref, out_ref):
    for q in range(out_ref.shape[1]):
        at = slice(q * LANES, (q + 1) * LANES)
        row = slice(q, q + 1)
        cell = cell_ref[:, at].astype(F32)
        line = jnp.floor((cell + 0.5) * (1.0 / tile_cols))
        out_ref[0, row, :] = cell - line * tile_cols
        out_ref[1, row, :] = innov_ref[:, at]
        out_ref[2, row, :] = weight_ref[:, at]
        out_ref[3, row, :] = level_ref[:, at].astype(F32) * tile_rows + line


def split(innovation, weight, cell, level, tile_rows, tile_cols):
    return pl.pallas_call(
        functools.partial(split_kernel, tile_rows, tile_cols),
        in_specs=[VMEM] * 4,
        out_specs=VMEM,
        out_shape=jax.ShapeDtypeStruct((4, cell.size // LANES, LANES), F32),
        name="split",
    )(innovation, weight, cell, level)


def pick_kernel(early_ref, pert_ref, out_ref, hot_ref, line_ref, flat_ref):
    levels, tile_rows, tile_cols = pert_ref.shape[1:]
    chunks = early_ref.shape[1]

    @pl.when(pl.program_id(0) == 0)
    def _():
        key = early_ref[3]
        level = jnp.zeros_like(key)
        for l in range(1, levels):
            level += jnp.where(key >= l * tile_rows, 1.0, 0.0)
        line_ref[...] = key - level * tile_rows
        place = early_ref[0] + level * tile_cols
        sub = lax.broadcasted_iota(jnp.int32, (levels * tile_cols, LANES), 0).astype(F32)
        for q in range(chunks):
            hot = jnp.where(sub == place[q : q + 1, :], 1.0, 0.0)
            hot_ref[:, q * LANES : (q + 1) * LANES] = hot.astype(BF16)

    for l in range(levels):
        flat_ref[:, l * tile_cols : (l + 1) * tile_cols] = pert_ref[0, l]
    rows = lax.broadcasted_iota(jnp.int32, (tile_rows, LANES), 0).astype(F32)
    for q in range(0, chunks, 2):
        lines = jnp.dot(
            flat_ref[...], hot_ref[:, q * LANES : (q + 2) * LANES], preferred_element_type=F32
        )
        for h in range(2):
            mine = lines[:, h * LANES : (h + 1) * LANES]
            kept = jnp.where(rows == line_ref[q + h : q + h + 1, :], mine, 0.0)
            out_ref[0, q + h : q + h + 1, :] = jnp.sum(kept, axis=0, keepdims=True)


def pick(perturbations, early):
    members, levels, tile_rows, tile_cols = perturbations.shape
    chunks = early.shape[1]
    return pl.pallas_call(
        pick_kernel,
        grid=(members,),
        in_specs=[
            pl.BlockSpec(early.shape, lambda m: (0, 0, 0)),
            pl.BlockSpec((1, levels, tile_rows, tile_cols), lambda m: (m, 0, 0, 0)),
        ],
        out_specs=pl.BlockSpec((1, chunks, LANES), lambda m: (m, 0, 0)),
        out_shape=jax.ShapeDtypeStruct((members, chunks, LANES), F32),
        scratch_shapes=[
            pltpu.VMEM((levels * tile_cols, chunks * LANES), BF16),
            pltpu.VMEM((chunks, LANES), F32),
            pltpu.VMEM((tile_rows, levels * tile_cols), BF16),
        ],
        name="pick",
    )(early, perturbations)


def take_row(row, index):
    return jnp.take_along_axis(
        jnp.broadcast_to(row, (8, LANES)), index, axis=1, mode="promise_in_bounds"
    )


def krylov_kernel(shift, own, line_rows, tile_cols, stacks, more, *refs):
    key_ref, table_ref, spec_ref = refs[:3]
    early_refs, pert_refs = refs[3 : 3 + stacks], refs[3 + stacks : 3 + stacks + more]
    rows_ref, moment_ref, base_ref, ext_ref, pairs_ref, t_ref, acc_ref, kept_ref = refs[3 + stacks + more :]
    members, chunks = own * len(pert_refs), early_refs[0].shape[2]
    levels = table_ref.shape[0]
    per_level = table_ref.shape[1] // LANES
    bands = levels * line_rows
    fields = 5 + members
    mirror = lax.axis_index("lon")
    KEY, COL, EDGE, YY, WW = 0, 1, 2, 3, 4

    count = jnp.sum(jnp.where(key_ref[...] < (bands << shift), 1.0, 0.0)).astype(jnp.int32)
    vregs = jnp.maximum((count + 8 * LANES - 1) // (8 * LANES), 1)
    depth = vregs * 8
    sub = lax.broadcasted_iota(jnp.int32, (8, LANES), 0)
    lane = lax.broadcasted_iota(jnp.int32, (8, LANES), 1)
    zero = jnp.zeros((8, LANES), F32)

    def load_sorted(v, carry):
        place = lane * depth + v * 8 + sub
        high, low = place >> 7, place & (LANES - 1)

        def key_step(g, found):
            for i in range(8):
                r = g * 8 + i
                found = jnp.where(high == r, take_row(key_ref[pl.ds(r, 1), :], low), found)
            return found

        key = lax.fori_loop(0, vregs, key_step, jnp.full((8, LANES), bands << shift, jnp.int32))
        inside = place < count
        band = key >> shift
        index = key & ((1 << shift) - 1)
        high, low = index >> 7, index & (LANES - 1)

        def slot_step(slot, tile, ref, t, found):
            offset = (tile * tile_cols).astype(F32)
            for q in range(chunks):
                here = high == slot * chunks + q
                rows = [ref[t, k, q : q + 1, :] for k in range(3)]
                rows[0] += offset
                rows += [pert[slot, m, q : q + 1, :] for pert in pert_refs for m in range(own)]
                found = tuple(jnp.where(here, take_row(row, low), f) for row, f in zip(rows, found))
            return found

        found = (zero,) * (3 + members)
        if len(early_refs) > 1:
            for slot, ref in enumerate(early_refs):
                found = slot_step(slot, mirror ^ slot, ref, 0, found)
        else:
            ref = early_refs[0]
            found = lax.fori_loop(0, ref.shape[0], lambda t, f: slot_step(t, t, ref, t, f), found)

        level = jnp.zeros((8, LANES), jnp.int32)
        for l in range(1, levels):
            level += jnp.where(band >= l * line_rows, 1, 0)
        col, innov, weight = found[:3]
        col_int = col.astype(jnp.int32)
        wave = KMAX * col_int
        turn = (wave - (wave // NLON) * NLON).astype(F32) * (2.0 * np.pi / NLON)
        scale = zero
        for l in range(levels):
            last = spec_ref[l : l + 1, 2 * KMAX - 1 :] * (1.0 / np.sqrt(KMAX))
            scale = jnp.where(level == l, jnp.broadcast_to(last, (8, LANES)), scale)
        at = pl.ds(v * 8, 8)
        base_ref[KEY, at, :] = band.astype(F32)
        base_ref[COL, at, :] = col
        base_ref[EDGE, at, :] = jnp.where(inside, jnp.sin(turn) * scale, 0.0)
        base_ref[YY, at, :] = jnp.where(inside, weight * innov, 0.0)
        base_ref[WW, at, :] = jnp.where(inside, weight, 0.0)
        for m in range(members):
            base_ref[5 + m, at, :] = jnp.where(inside, found[3 + m], 0.0)
        pairs_ref[at, :] = level * per_level
        return carry

    lax.fori_loop(0, vregs, load_sorted, 0)

    def next_lane(x):
        return jnp.where(lane == LANES - 1, 0.0, pltpu.roll(x, LANES - 1, 1))

    def clear(v, carry):
        acc_ref[pl.ds(v * 8, 8), :] = zero
        acc_ref[pl.ds(depth + v * 8, 8), :] = zero
        return carry

    def fold(target, turns):
        def one(v, carry):
            at, beyond = pl.ds(v * 8, 8), pl.ds(depth + v * 8, 8)
            t_ref[target, at, :] += pltpu.roll(acc_ref[at, :], turns, 1) + pltpu.roll(
                acc_ref[beyond, :], turns + 1, 1
            )
            return carry

        lax.fori_loop(0, vregs, one, 0)

    def apply(target):
        def fill(v, carry):
            at, beyond = pl.ds(v * 8, 8), pl.ds(depth + v * 8, 8)
            for f in range(fields):
                value = base_ref[f, at, :]
                ext_ref[f, at, :] = value
                ext_ref[f, beyond, :] = next_lane(value)
            t_ref[target, at, :] = zero
            return carry

        lax.fori_loop(0, vregs, fill, 0)

        def lap(state):
            turns, going, _ = state
            lax.fori_loop(0, vregs, clear, 0)

            def batch(state):
                start, _ = state

                def one(v, hit):
                    at = pl.ds(v * 8, 8)
                    mine = [base_ref[f, at, :] for f in range(fields)]
                    chunk = pairs_ref[at, :]
                    total = t_ref[target, at, :]
                    for b in range(8):
                        there = pl.ds(start + b + v * 8, 8)
                        other = [ext_ref[f, there, :] for f in range(fields)]
                        same = mine[KEY] == other[KEY]
                        lag = jnp.abs(mine[COL] - other[COL]).astype(jnp.int32)
                        lag = jnp.minimum(lag, NLON - lag)
                        which = chunk + (lag >> 7)
                        low = lag & (LANES - 1)
                        value = zero
                        for e in range(levels * per_level):
                            l, k = divmod(e, per_level)
                            row = table_ref[l : l + 1, k * LANES : (k + 1) * LANES]
                            value = jnp.where(which == e, take_row(row, low), value)
                        value += mine[EDGE] * other[EDGE]
                        weight = mine[5] * other[5]
                        for m in range(1, members):
                            weight += mine[5 + m] * other[5 + m]
                        value = jnp.where(same, value * weight, 0.0)
                        kept_ref[jnp.minimum(start, KEPT) + b, at, :] = value
                        total += value * other[YY]
                        first = (turns == 0) & (start + b == 0)
                        acc_ref[there, :] += value * mine[YY] * jnp.where(first, 0.0, 1.0)
                        if b == 7:
                            hit = jnp.maximum(hit, jnp.where(same & (mine[KEY] < bands), 1.0, 0.0))
                    t_ref[target, at, :] = total
                    return hit

                hit = lax.fori_loop(0, vregs, one, zero)
                return start + 8, jnp.max(hit) > 0.5

            end, going = lax.while_loop(lambda s: (s[0] < depth) & s[1], batch, (0, going))
            fold(target, turns)

            @pl.when(going)
            def _():
                def advance(v, carry):
                    spots = [
                        (f, pl.ds(at + v * 8, 8)) for f in range(fields) for at in (0, depth)
                    ]
                    values = [next_lane(ext_ref[f, at, :]) for f, at in spots]
                    for (f, at), value in zip(spots, values):
                        ext_ref[f, at, :] = value
                    return carry

                lax.fori_loop(0, vregs, advance, 0)

            return turns + 1, going, end

        turns, _, end = lax.while_loop(
            lambda s: (s[0] < LANES - 1) & s[1], lap, (0, True, 0)
        )
        return turns, end

    def apply_kept(target, end):
        lax.fori_loop(0, vregs, clear, 0)

        def fill(v, carry):
            at = pl.ds(v * 8, 8)
            value = base_ref[YY, at, :]
            ext_ref[YY, at, :] = value
            ext_ref[YY, pl.ds(depth + v * 8, 8), :] = next_lane(value)
            t_ref[target, at, :] = zero
            return carry

        lax.fori_loop(0, vregs, fill, 0)

        def batch(g, carry):
            def one(v, carry):
                at = pl.ds(v * 8, 8)
                mine = base_ref[YY, at, :]
                total = t_ref[target, at, :]
                for b in range(8):
                    there = pl.ds(g * 8 + b + v * 8, 8)
                    value = kept_ref[g * 8 + b, at, :]
                    total += value * ext_ref[YY, there, :]
                    acc_ref[there, :] += value * mine * jnp.where(g * 8 + b == 0, 0.0, 1.0)
                t_ref[target, at, :] = total
                return carry

            return lax.fori_loop(0, vregs, one, carry)

        lax.fori_loop(0, end // 8, batch, 0)
        fold(target, 0)

    turns, end = apply(0)

    def middle(v, carry):
        at = pl.ds(v * 8, 8)
        t_ref[2, at, :] = base_ref[YY, at, :]
        base_ref[YY, at, :] = base_ref[WW, at, :] * t_ref[0, at, :]
        return carry

    lax.fori_loop(0, vregs, middle, 0)
    kept = (turns == 1) & (end <= KEPT)

    @pl.when(kept)
    def _():
        apply_kept(1, end)

    @pl.when(jnp.logical_not(kept))
    def _():
        apply(1)

    def products(v, sums):
        at = pl.ds(v * 8, 8)
        y0, y1 = t_ref[2, at, :], base_ref[YY, at, :]
        t0, t1 = t_ref[0, at, :], t_ref[1, at, :]
        y2 = base_ref[WW, at, :] * t1
        t_ref[3, at, :] = y2
        return sums[0] + y0 * t0, sums[1] + y0 * t1, sums[2] + y1 * t1, sums[3] + y2 * t1

    sums = lax.fori_loop(0, vregs, products, (zero,) * 4)
    moments = jnp.concatenate(
        [jnp.sum(s, axis=0, keepdims=True) for s in sums] + [jnp.zeros((4, LANES), F32)]
    )
    for g in range(moment_ref.shape[0]):
        moment_ref[g] = moments

    def unload(v, carry):
        place = (v * 8 + sub) * LANES + lane
        column = jnp.floor((place.astype(F32) + 0.5) / depth.astype(F32)).astype(jnp.int32)
        column = jnp.minimum(column, LANES - 1)
        row = place - column * depth

        def step(g, found):
            for i in range(8):
                r = g * 8 + i
                here = row == r
                at = pl.ds(r, 1)
                rows = [base_ref[COL, at, :]] + [base_ref[5 + m, at, :] for m in range(own)]
                rows += [t_ref[2, at, :], base_ref[YY, at, :], t_ref[3, at, :]]
                found = tuple(jnp.where(here, take_row(r_, column), f) for r_, f in zip(rows, found))
            return found

        found = lax.fori_loop(0, vregs, step, (zero,) * (4 + own))
        for f, value in enumerate(found):
            rows_ref[f, pl.ds(v * 8, 8), :] = value
        return carry

    lax.fori_loop(0, vregs, unload, 0)


def krylov(keys, early, pert, table, spectrum, shift, own, line_rows, tile_cols, copies):
    members = own * len(pert)
    sources = keys.shape[0]
    fields = 5 + members
    return pl.pallas_call(
        functools.partial(krylov_kernel, shift, own, line_rows, tile_cols, len(early), len(pert)),
        in_specs=[VMEM] * (3 + len(early) + len(pert)),
        out_specs=[VMEM] * 2,
        out_shape=[
            jax.ShapeDtypeStruct((4 + own, sources, LANES), F32),
            jax.ShapeDtypeStruct((copies, 8, LANES), F32),
        ],
        scratch_shapes=[
            pltpu.VMEM((fields, sources, LANES), F32),
            pltpu.VMEM((fields, 2 * sources + 8, LANES), F32),
            pltpu.VMEM((sources, LANES), jnp.int32),
            pltpu.VMEM((4, sources, LANES), F32),
            pltpu.VMEM((2 * sources + 8, LANES), F32),
            pltpu.VMEM((KEPT + 8, sources, LANES), F32),
        ],
        name="krylov",
    )(keys, table, spectrum, *early, *pert)


def halves(value):
    high = value.astype(BF16)
    return high, (value - high.astype(F32)).astype(BF16)


def expand_kernel(
    shift, own, line_rows, chunk,
    skey_ref, key_ref, rows_ref, moment_ref, spec_ref, sol_ref, res_ref, trig_ref, basis_ref,
):
    levels = spec_ref.shape[0]
    bands = levels * line_rows

    def total(i):
        lanes = jnp.sum(moment_ref[:, i, :], axis=0, keepdims=True)
        return jnp.broadcast_to(jnp.sum(lanes, axis=1, keepdims=True), (1, LANES))

    m0, m1, m2, m3 = (total(i) for i in range(4))
    step0 = m0 / (m0 + m1)
    keep = 1.0 - step0
    next_norm = keep * keep * m0 - 2.0 * keep * step0 * m1 + step0 * step0 * m2
    ratio = next_norm / m0
    u, v = keep + ratio, -step0
    curvature = u * u * m0 + (2.0 * u * v + u * u) * m1 + (2.0 * u * v + v * v) * m2 + v * v * m3
    step1 = next_norm / curvature
    sol_c = (step0 + step1 * u, step1 * v)
    res_c = (keep - step1 * u, -step0 - step1 * (u + v), -step1 * v)

    count = jnp.sum(jnp.where(key_ref[...] < (bands << shift), 1.0, 0.0)).astype(jnp.int32)
    sol_ref[...] = jnp.zeros_like(sol_ref)
    res_ref[...] = jnp.zeros_like(res_ref)
    per = BLOCK // LANES
    steps = lax.broadcasted_iota(jnp.int32, (8, BLOCK), 0).astype(F32)
    leaps = lax.broadcasted_iota(jnp.int32, (KMAX // 8, BLOCK), 0).astype(F32) * 8.0

    def block(p, carry):
        def lanes(get):
            return jnp.concatenate([get(p * per + i) for i in range(per)], axis=1)

        def field(f):
            return lanes(lambda i: rows_ref[f, pl.ds(i, 1), :])

        place = lax.broadcasted_iota(jnp.int32, (1, BLOCK), 1) + p * BLOCK
        inside = place < count
        band = lanes(lambda i: key_ref[pl.ds(i, 1), :]) >> shift
        col = jnp.where(inside, field(0), 0.0)
        y0, y1, y2 = (field(1 + own + k) for k in range(3))
        wider = lambda c: jnp.concatenate([c] * per, axis=1)
        sol_y = wider(sol_c[0]) * y0 + wider(sol_c[1]) * y1
        res_y = wider(res_c[0]) * y0 + wider(res_c[1]) * y1 + wider(res_c[2]) * y2
        coefs = []
        for y in (sol_y, res_y):
            for m in range(own):
                coefs.append(halves(jnp.where(inside, field(1 + m) * y, 0.0)))

        for part, value in enumerate(cos_sin(col, leaps)):
            trig_ref[part] = value
        near = cos_sin(col, steps)
        after = cos_sin(col, steps + 1.0)
        for c in range(0, 2 * KMAX, 16):
            waves = []
            for a in ((c % KMAX) // 8, (c % KMAX) // 8 + 1):
                far_cos, far_sin = trig_ref[0, a : a + 1, :], trig_ref[1, a : a + 1, :]
                if c < KMAX:
                    waves.append(far_cos * near[0] - far_sin * near[1])
                else:
                    waves.append(far_sin * after[0] + far_cos * after[1])
            high, low = halves(jnp.concatenate(waves, axis=0))
            basis_ref[c : c + 16, :BLOCK] = high
            basis_ref[c : c + 16, BLOCK : 2 * BLOCK] = high
            basis_ref[c : c + 16, 2 * BLOCK :] = low

        first = skey_ref[p * BLOCK] >> shift
        last = skey_ref[jnp.minimum(p * BLOCK + BLOCK, count) - 1] >> shift

        def strip(g, carry):
            rows = lax.broadcasted_iota(jnp.int32, (chunk, BLOCK), 0) + g * chunk
            hit = rows == band

            def spot(part):
                return jnp.where(hit, part.astype(F32), 0.0)

            left_high = jnp.concatenate([spot(c[0]) for c in coefs], axis=0).astype(BF16)
            left_low = jnp.concatenate([spot(c[1]) for c in coefs], axis=0).astype(BF16)
            left = jnp.concatenate([left_high, left_low, left_high], axis=1)
            lines = lax.dot_general(
                left, basis_ref[...], (((1,), (1,)), ((), ())), preferred_element_type=F32
            )
            at = pl.ds(pl.multiple_of(g * chunk, 8), chunk)
            for k in range(2 * own):
                out = sol_ref if k < own else res_ref
                out[k % own, at, :] += lines[k * chunk : (k + 1) * chunk]
            return carry

        lax.fori_loop(first // chunk, last // chunk + 1, strip, 0)
        return carry

    lax.fori_loop(0, (count + BLOCK - 1) // BLOCK, block, 0)
    for out in (sol_ref, res_ref):
        for m in range(own):
            for l in range(levels):
                at = slice(l * line_rows, (l + 1) * line_rows)
                out[m, at, :] = out[m, at, :] * (spec_ref[l : l + 1, :] / np.sqrt(KMAX))


def expand(keys, rows, moments, spectrum, shift, own, line_rows):
    bands = spectrum.shape[0] * line_rows
    chunk = min(64, -(-bands // 16) * 16)
    padded = -(-bands // chunk) * chunk
    outs = pl.pallas_call(
        functools.partial(expand_kernel, shift, own, line_rows, chunk),
        in_specs=[SMEM] + [VMEM] * 4,
        out_specs=[VMEM] * 2,
        out_shape=[jax.ShapeDtypeStruct((own, padded, 2 * KMAX), F32)] * 2,
        scratch_shapes=[
            pltpu.VMEM((2, KMAX // 8, BLOCK), F32),
            pltpu.VMEM((2 * KMAX, 3 * BLOCK), BF16),
        ],
        name="expand",
    )(keys.reshape(-1), keys, rows, moments, spectrum)
    return tuple(o[:, :bands].reshape(own, -1, line_rows, 2 * KMAX) for o in outs)


def body(perturbations, innovation, obs_weight, obs_cell, obs_level, cutoff):
    own, levels, tile_rows, tile_cols = perturbations.shape
    line_rows = tile_rows // lax.axis_size("lon")
    flat = obs_cell.size
    padding = -flat % BLOCK
    inputs = (innovation, obs_weight, obs_cell, obs_level)
    if padding:
        inputs = (jnp.pad(x.reshape(1, -1), ((0, 0), (0, padding))) for x in inputs)
    early = split(*inputs, tile_rows, tile_cols)
    picked = pick(perturbations, early)
    along = spread(jnp.concatenate([early, picked]), "lon")
    pert = all_members(jnp.concatenate([a[:, early.shape[0] :] for a in along]))
    spectrum, table = tables(cutoff)

    shift = (lax.axis_size("lon") * (flat + padding) - 1).bit_length()
    keys = sort_keys(along, shift, flat, levels, tile_rows, line_rows)
    keys = lax.sort(keys.reshape(-1), is_stable=False).reshape(-1, LANES)
    groups = lax.axis_size("lat") * lax.axis_size("lon")
    direct = groups <= 16
    rows, moments = krylov(
        keys, along, pert, table, spectrum,
        shift, own, line_rows, tile_cols, groups if direct else 1,
    )
    if direct:
        moments = lax.all_to_all(moments, ("lat", "lon"), 0, 0, tiled=True)
    else:
        moments = lax.psum(moments, ("lat", "lon"))
    return expand(keys, rows, moments, spectrum, shift, own, line_rows)


def solution(mesh):
    placed = (
        P("mem", None, "lat", "lon"),
        P("lat", "lon"),
        P("lat", "lon"),
        P("lat", "lon"),
        P("lat", "lon"),
        P(),
    )
    return jax.shard_map(
        body,
        mesh=mesh,
        in_specs=placed,
        out_specs=(P("mem", None, ("lat", "lon"), None), P("mem", None, ("lat", "lon"), None)),
        check_vma=False,
    )
```
